256 devices in a mesh: subj: 8 (over z_hi, core), slab: 32 (over y, z_lo, x).
Axes of the slice: x: 4, y: 4, z: 8 (z_hi: 4, z_lo: 2; z = z_hi * 2 + z_lo), core: 2. Of those that a mesh axis runs over, the one named last changes fastest.
Arguments:
- template: float32 [128, 128, 512], P('slab', 'subj'), may hold values from -6 to 6
- subject: float32 [8, 128, 128, 512], P('subj', 'slab'), may hold values from -6 to 6
- velocity: float32 [8, 2, 3, 128, 128, 512], P('subj', None, None, 'slab'), may hold values from -0.6 to 0.6
Outputs:
- velocity_grad: float32 [8, 2, 3, 128, 128, 512], P('subj', None, None, 'slab')
- template_grad: float32 [128, 128, 512], P('slab', 'subj')
The draws below stay inside these ranges and needn't reach their ends.
All inputs are finite; a program needn't handle non-finite values.
Results may differ from the reference program's by a relative error of at most 0.0003.
Values sent between devices are 32-bit elements; how exact they have to be, the bound alone decides.
A program may use at most 128 MiB of HBM per device.

```python
import jax
import jax.numpy as jnp
from jax import lax

NY = 128
NX = 512
TS = 2
SW = 3
NSUBJ = 8
NZ = 128


def block_scale(own_key, dims, cuts, least, largest):
    loudness, own = 1.0, jax.random.fold_in(own_key, 6)
    for dim, shards_of in cuts:
        steps = jnp.exp(jax.random.uniform(jax.random.fold_in(own, dim), (shards_of,), jnp.float32, least / len(cuts), largest / len(cuts)))
        loudness = loudness * jnp.repeat(steps, dims[dim] // shards_of).reshape([-1 if axis == dim else 1 for axis in range(len(dims))])
    return loudness


def scatter_about(own_key, dims, deviation, limit, cuts=(), kind=jnp.bfloat16):
    drawn = jax.random.normal(own_key, dims, jnp.float32) * deviation
    if len(cuts) > 0:
        drawn = block_scale(own_key, dims, cuts, -0.22, 0.18) * drawn
    return jnp.clip(drawn, min=-limit, max=limit).astype(kind)


def setup_inputs(seed: int = 0) -> dict:
    splits = jax.random.split(jax.random.key(seed), 4)
    template = scatter_about(splits[0], (NZ, NY, NX), 1.0, 6.0, ((0, 32), (1, 8)), jnp.float32)
    subject = scatter_about(splits[1], (NSUBJ, NZ, NY, NX), 1.0, 6.0, ((0, 8), (1, 32)), jnp.float32)
    velocity = jnp.clip(jax.random.uniform(splits[2], (NSUBJ, TS, 3, NZ, NY, NX), jnp.float32, -0.6, 0.6) * block_scale(splits[2], (NSUBJ, TS, 3, NZ, NY, NX), ((0, 8), (3, 32)), -0.4, 0.0), -0.6, 0.6)
    return dict(template=template, subject=subject, velocity=velocity)


smooth_weight = 1.0
match_weight = 5.0


def shifted(field, dimension, offset):
    widths = [(0, 0)] * field.ndim
    widths[dimension] = (1, 1)
    padded = jnp.pad(field, widths)
    length = field.shape[dimension]
    return lax.slice_in_dim(padded, 1 + offset, 1 + offset + length, axis=dimension)


def neighbours(field):
    total = jnp.zeros_like(field)
    for dimension in range(field.ndim - 3, field.ndim):
        total = total + shifted(field, dimension, 1) + shifted(field, dimension, -1)
    return total


def smooth(source):
    scale = 1.0 + 6.0 * smooth_weight
    smoothed = source / scale
    for sweep_index in range(SW - 1):
        smoothed = (source + smooth_weight * neighbours(smoothed)) / scale
    return smoothed


def one_subject(template, subject_image, flow_field):
    step_size = 1.0 / TS
    image = template
    saved = []
    for step_index in range(TS):
        flow_step = flow_field[step_index]
        back_diffs = [image - shifted(image, dimension, -1) for dimension in range(3)]
        fore_diffs = [shifted(image, dimension, 1) - image for dimension in range(3)]
        saved.append((back_diffs, fore_diffs))
        flux = jnp.zeros_like(image)
        for dimension in range(3):
            flux = flux + jnp.maximum(flow_step[dimension], 0.0) * back_diffs[dimension] + jnp.minimum(flow_step[dimension], 0.0) * fore_diffs[dimension]
        image = image - step_size * flux
    adjoint = image - subject_image
    sources = [None] * TS
    for step_index in reversed(range(TS)):
        flow_step = flow_field[step_index]
        back_diffs, fore_diffs = saved[step_index]
        sources[step_index] = jnp.stack([-match_weight * step_size * adjoint * jnp.where(flow_step[dimension] >= 0.0, back_diffs[dimension], fore_diffs[dimension]) for dimension in range(3)])
        total = jnp.zeros_like(adjoint)
        for dimension in range(3):
            positive = jnp.maximum(flow_step[dimension], 0.0) * adjoint
            negative = jnp.minimum(flow_step[dimension], 0.0) * adjoint
            total = total + (positive - shifted(positive, dimension, 1)) + (shifted(negative, dimension, -1) - negative)
        adjoint = adjoint - step_size * total
    source = jnp.stack(sources)
    return flow_field + smooth(source), adjoint


def reference(template, subject, velocity):
    gradients = []
    summed = jnp.zeros_like(template)
    for subject_index in range(NSUBJ):
        gradient, adjoint = one_subject(template, subject[subject_index], velocity[subject_index])
        gradients.append(gradient)
        summed = summed + adjoint
    return jnp.stack(gradients), summed
```

```python
import functools

import jax
import jax.numpy as jnp
from jax import lax
from jax.experimental import pallas as pl
from jax.experimental.pallas import tpu as pltpu
from jax.sharding import PartitionSpec as P

MESH = pl.DeviceIdType.MESH
F32 = jnp.float32
DT = 0.5
WEIGHT = -2.5
SEVENTH = 1.0 / 7.0
PAD = 8
R = 16


def kernel(
    nslab, tmpl, subj, vel, out, tg,
    T, I1, L2, L1, S, U, V, V0H, SUB, FS, FR, A0, RB, PS, RZ, TG,
    xs, xr, ts, tr, rs, rr, ls,
):
    ny, nx = tmpl.shape[1] * 8, tmpl.shape[2]
    blk = tmpl.shape[1]
    half = blk // 2
    nchunk = ny // R
    g = lax.axis_index("subj")
    s = lax.axis_index("slab")
    q, c = g // 2, lax.rem(g, 2)
    sib = g + 1 - 2 * c
    has_up, has_dn = s < nslab - 1, s > 0

    def ring(k):
        return 2 * lax.rem(q + k, 4) + c

    def rows(b, n=blk):
        return pl.ds(pl.multiple_of(PAD + b, 8), n)

    body = pl.ds(PAD, ny)
    loads = []
    for t in range(2):
        for d in range(3):
            loads.append(pltpu.make_async_copy(vel.at[0, t, d], V.at[t, d, :, body], ls.at[3 * t + d]))
    loads.append(pltpu.make_async_copy(subj.at[0], SUB, ls.at[6]))
    loads.append(pltpu.make_async_copy(tmpl, T.at[pl.ds(0, 4), rows(g * blk)], ls.at[7]))
    for copy in (loads[7], loads[0], loads[1], loads[2], loads[3], loads[4], loads[5], loads[6]):
        copy.start()

    barrier = pltpu.get_barrier_semaphore()

    def greet(**where):
        pl.semaphore_signal(barrier, inc=1, device_id=where, device_id_type=MESH)

    for peer in (sib, ring(1), ring(2), ring(3)):
        greet(subj=peer)

    greet(slab=lax.rem(s + 1, nslab))
    greet(slab=lax.rem(s + nslab - 1, nslab))

    edge = jnp.zeros((PAD, nx), F32)

    def zero_pads(ref, count):
        def step(p, _):
            ref[p, pl.ds(0, PAD)] = edge
            ref[p, pl.ds(PAD + ny, PAD)] = edge
            return 0

        lax.fori_loop(0, count, step, 0)

    zero_pads(T, 8)
    zero_pads(I1, 6)
    zero_pads(L2, 4)
    zero_pads(L1, 6)
    zero_pads(U, 6)
    for t in range(2):
        zero_pads(V.at[t, 1], 4)
        for d in range(3):
            zero_pads(S.at[t, d], 8)

    def zero_plane(ref, first=0):
        def step(i, _):
            ref[pl.ds(pl.multiple_of(first + i * R, 8), R)] = jnp.zeros((R, nx), F32)
            return 0

        lax.fori_loop(0, nchunk, step, 0)

    def zero_side(side):
        planes, seconds, firsts = ((6, 7), 0, 1) if side == 0 else ((4, 5), 7, 6)
        for p in planes:
            T[p, rows(g * blk)] = jnp.zeros((blk, nx), F32)
        for d in range(3):
            zero_plane(V0H.at[side, d])
            zero_plane(S.at[1, d, seconds], PAD)
            zero_plane(S.at[1, d, firsts], PAD)
            zero_plane(S.at[0, d, seconds], PAD)
        zero_plane(FR.at[side])
        zero_plane(L1.at[0 if side == 0 else 5], PAD)
        zero_plane(U.at[0 if side == 0 else 5], PAD)

    @pl.when(s == 0)
    def _():
        zero_side(0)

    @pl.when(s == nslab - 1)
    def _():
        zero_side(1)

    pl.semaphore_wait(barrier, 6)

    def xcopy(k, dirn):
        up = dirn == 0
        if k == 0:
            src = tmpl.at[pl.ds(2 if up else 0, 2)]
            dst = T.at[pl.ds(6 if up else 4, 2), rows(g * blk)]
        elif k < 4:
            src, dst = vel.at[0, 0, k - 1, 3 if up else 0], V0H.at[dirn, k - 1]
        elif k < 7:
            src, dst = S.at[1, k - 4, 4 if up else 3, body], S.at[1, k - 4, 0 if up else 7, body]
        elif k == 7:
            src, dst = FS.at[dirn], FR.at[dirn]
        elif k < 11:
            src, dst = S.at[1, k - 8, 5 if up else 2, body], S.at[1, k - 8, 1 if up else 6, body]
        elif k == 11:
            src, dst = L1.at[4 if up else 1, body], L1.at[0 if up else 5, body]
        else:
            src, dst = S.at[0, k - 12, 4 if up else 3, body], S.at[0, k - 12, 0 if up else 7, body]
        return pltpu.make_async_remote_copy(
            src, dst, xs.at[dirn, k], xr.at[dirn, k],
            device_id={"slab": s + 1 if up else s - 1}, device_id_type=MESH)

    def xstart(ks):
        @pl.when(has_up)
        def _():
            for k in ks:
                xcopy(k, 0).start()

        @pl.when(has_dn)
        def _():
            for k in ks:
                xcopy(k, 1).start()

    def xrecv(ks):
        @pl.when(has_dn)
        def _():
            for k in ks:
                xcopy(k, 0).wait_recv()

        @pl.when(has_up)
        def _():
            for k in ks:
                xcopy(k, 1).wait_recv()

    def xsent(ks):
        @pl.when(has_up)
        def _():
            for k in ks:
                xcopy(k, 0).wait_send()

        @pl.when(has_dn)
        def _():
            for k in ks:
                xcopy(k, 1).wait_send()

    def tcopy(ph, k, recv=False):
        owner = {0: g, 1: g, 2: ring(3), 3: ring(1), 4: g, 5: ring(3), 6: ring(1), 7: ring(2), 8: ring(2)}[k]
        if recv:
            owner = {0: ring(3), 1: ring(1), 2: ring(2), 3: ring(2)}.get(k, owner + 1 - 2 * c if k > 3 else None)
        off, n = {2: (0, half), 3: (half, half), 7: (0, half), 8: (half, half)}.get(k, (0, blk))
        place = T.at[pl.ds(4 * ph, 4), rows(owner * blk + off, n)]
        src = tmpl if (ph == 0 and k in (0, 1, 4)) else place
        peer = {0: ring(1), 1: ring(3), 2: ring(1), 3: ring(3)}.get(k, sib)
        return pltpu.make_async_remote_copy(
            src, place, ts.at[ph, k], tr.at[ph, k], device_id={"subj": peer}, device_id_type=MESH)

    def twait(ph, k):
        tcopy(ph, k, True).wait_recv()

    xstart((0,))
    for k in (0, 1, 4):
        tcopy(0, k).start()
    xstart((1, 2, 3))
    xrecv((0,))
    for k in (0, 1, 4):
        tcopy(1, k).start()
    for ph in range(2):
        twait(ph, 0)
        tcopy(ph, 2).start()
        tcopy(ph, 5).start()
        twait(ph, 1)
        tcopy(ph, 3).start()
        tcopy(ph, 6).start()
        twait(ph, 2)
        tcopy(ph, 7).start()
        twait(ph, 3)
        tcopy(ph, 8).start()
    for ph in range(2):
        for k in (4, 5, 6, 7, 8):
            twait(ph, k)

    lane = lax.broadcasted_iota(jnp.int32, (R, 128), 1)
    first_lane, last_lane = lane == 0, lane == 127

    def left(x):
        y = pltpu.roll(x, 1, 1)
        return jnp.concatenate([jnp.where(first_lane, 0.0, y[:, :128]), y[:, 128:]], axis=1)

    def right(x):
        y = pltpu.roll(x, nx - 1, 1)
        return jnp.concatenate([y[:, : nx - 128], jnp.where(last_lane, 0.0, y[:, nx - 128 :])], axis=1)

    def chunks(fn):
        def step(i, _):
            fn(pl.multiple_of(i * R, R))
            return 0

        lax.fori_loop(0, nchunk, step, 0)

    def at(ref, r):
        return ref[pl.ds(pl.multiple_of(PAD + r, 8), R)]

    def flat(ref, r):
        return ref[pl.ds(r, R)]

    def around(ref, r):
        ext = ref[pl.ds(r, R + 16)]
        n = R + 16
        return ext[8 : 8 + R], pltpu.roll(ext, 1, 0)[8 : 8 + R], pltpu.roll(ext, n - 1, 0)[8 : 8 + R]

    def put(ref, r, x):
        ref[pl.ds(pl.multiple_of(PAD + r, 8), R)] = x

    def advect(plane, below, above, vread, r):
        here, ym, yp = around(plane, r)
        pairs = ((at(below, r), at(above, r)), (ym, yp), (left(here), right(here)))
        diffs, total = [], None
        for d, (minus, plus) in enumerate(pairs):
            v = vread(d, r)
            diff = jnp.where(v >= 0.0, here - minus, plus - here)
            diffs.append(diff)
            total = v * diff if total is None else total + v * diff
        return here - DT * total, diffs

    def forward_0(z):
        if 0 <= z < 4:
            vread = lambda d, r: at(V.at[0, d, z], r)
        else:
            vread = lambda d, r: flat(V0H.at[0 if z < 0 else 1, d], r)

        def fn(r):
            new, diffs = advect(T.at[z % 8], T.at[(z - 1) % 8], T.at[(z + 1) % 8], vread, r)
            put(I1.at[z + 1], r, new)
            for d in range(3):
                put(S.at[0, d, z + 2], r, WEIGHT * diffs[d])

        chunks(fn)

    def forward_1(z):
        def fn(r):
            vread = lambda d, r: at(V.at[1, d, z], r)
            new, diffs = advect(I1.at[z + 1], I1.at[z], I1.at[z + 2], vread, r)
            lam = new - flat(SUB.at[z], r)
            put(L2.at[z], r, lam)
            scaled = WEIGHT * lam
            for d in range(3):
                put(S.at[1, d, z + 2], r, scaled * diffs[d])
            if z == 0:
                FS[1, pl.ds(r, R)] = jnp.maximum(vread(0, r), 0.0) * lam
            if z == 3:
                FS[0, pl.ds(r, R)] = jnp.minimum(vread(0, r), 0.0) * lam

        chunks(fn)

    def backward(t, lam_ref, z, below, above, r):
        lam = at(lam_ref, r)
        vz = at(V.at[t, 0, z], r)
        total = jnp.abs(vz) * lam - above(r) + below(r)
        vy, lam_ext = V[t, 1, z, pl.ds(r, R + 16)], lam_ref[pl.ds(r, R + 16)]
        pos, neg = jnp.maximum(vy, 0.0) * lam_ext, jnp.minimum(vy, 0.0) * lam_ext
        n = R + 16
        total = total + ((pos - neg)[8 : 8 + R] - pltpu.roll(pos, n - 1, 0)[8 : 8 + R] + pltpu.roll(neg, 1, 0)[8 : 8 + R])
        vx = at(V.at[t, 2, z], r)
        pos, neg = jnp.maximum(vx, 0.0) * lam, jnp.minimum(vx, 0.0) * lam
        total = total + ((pos - neg) - right(pos) + left(neg))
        return lam - DT * total

    def backward_1(z):
        def below(r):
            if z == 0:
                return flat(FR.at[0], r)
            return jnp.minimum(at(V.at[1, 0, z - 1], r), 0.0) * at(L2.at[z - 1], r)

        def above(r):
            if z == 3:
                return flat(FR.at[1], r)
            return jnp.maximum(at(V.at[1, 0, z + 1], r), 0.0) * at(L2.at[z + 1], r)

        def fn(r):
            lam = backward(1, L2.at[z], z, below, above, r)
            put(L1.at[z + 1], r, lam)
            for d in range(3):
                put(S.at[0, d, z + 2], r, at(S.at[0, d, z + 2], r) * lam)

        chunks(fn)

    def backward_0(z):
        def below(r):
            v = flat(V0H.at[0, 0], r) if z == 0 else at(V.at[0, 0, z - 1], r)
            return jnp.minimum(v, 0.0) * at(L1.at[z], r)

        def above(r):
            v = flat(V0H.at[1, 0], r) if z == 3 else at(V.at[0, 0, z + 1], r)
            return jnp.maximum(v, 0.0) * at(L1.at[z + 2], r)

        def fn(r):
            A0[z, pl.ds(r, R)] = backward(0, L1.at[z + 1], z, below, above, r)

        chunks(fn)

    def smooth(t, d):
        def sweep(p, low, high, r):
            here, ym, yp = around(S.at[t, d, p], r)
            beside = ym + yp + left(here) + right(here)
            if low:
                beside = beside + at(S.at[t, d, p - 1], r)
            if high:
                beside = beside + at(S.at[t, d, p + 1], r)
            put(U.at[p - 1], r, (here + beside * SEVENTH) * SEVENTH)

        def inner(p, _):
            chunks(lambda r: sweep(p, True, True, r))
            return 0

        lax.fori_loop(2, 6, inner, 0)

        @pl.when(has_dn)
        def _():
            chunks(lambda r: sweep(1, t == 1, True, r))

        @pl.when(has_up)
        def _():
            chunks(lambda r: sweep(6, True, t == 1, r))

        def last(z, _):
            def fn(r):
                here, ym, yp = around(U.at[z + 1], r)
                beside = ym + yp + left(here) + right(here) + at(U.at[z], r) + at(U.at[z + 2], r)
                put(V.at[t, d, z], r, at(V.at[t, d, z], r) + (at(S.at[t, d, z + 2], r) + beside) * SEVENTH)

            chunks(fn)
            return 0

        lax.fori_loop(0, 4, last, 0)

    def store(t, d):
        return pltpu.make_async_copy(V.at[t, d, :, body], out.at[0, t, d], ls.at[3 * t + d])

    for copy in loads:
        copy.wait()
    for z in range(4):
        forward_0(z)
    forward_1(1)
    forward_1(2)
    xstart((4, 5, 6))
    xrecv((1, 2, 3))
    forward_0(-1)
    forward_0(4)
    forward_1(0)
    forward_1(3)
    xstart((7, 8, 9, 10))
    backward_1(1)
    backward_1(2)
    xrecv((7,))
    backward_1(0)
    backward_1(3)
    xstart((11, 12, 13, 14))
    xrecv((4, 5, 6, 8, 9, 10))

    def smooth_1(d, _):
        smooth(1, d)
        return 0

    lax.fori_loop(0, 3, smooth_1, 0)
    for d in range(3):
        store(1, d).start()
    xrecv((11,))

    for z in range(4):
        backward_0(z)

    def pcopy(k):
        return pltpu.make_async_remote_copy(
            A0.at[:, pl.ds(pl.multiple_of((2 * k + 1 - c) * blk, 8), blk)], RB.at[k], rs.at[k], rr.at[k],
            device_id={"subj": sib}, device_id_type=MESH)

    for k in range(4):
        pcopy(k).start()

    def scale_halo(p, l):
        def fn(r):
            lam = at(L1.at[l], r)
            for d in range(3):
                put(S.at[0, d, p], r, at(S.at[0, d, p], r) * lam)

        chunks(fn)

    scale_halo(1, 0)
    scale_halo(6, 5)
    for k in range(4):
        pcopy(k).wait_recv()

    def pair_sum(k, _):
        for z in range(4):
            PS[k, z] = A0[z, pl.ds(pl.multiple_of((2 * k + c) * blk, 8), blk)] + RB[k, z]
        return 0

    lax.fori_loop(0, 4, pair_sum, 0)

    def zcopy(j):
        return pltpu.make_async_remote_copy(
            PS.at[lax.rem(q + j, 4)], RZ.at[j - 1], rs.at[3 + j], rr.at[3 + j],
            device_id={"subj": ring(j)}, device_id_type=MESH)

    for j in (2, 1, 3):
        zcopy(j).start()

    def smooth_0(d, _):
        smooth(0, d)
        return 0

    lax.fori_loop(0, 3, smooth_0, 0)
    for j in (1, 3, 2):
        zcopy(j).wait_recv()
    for z in range(4):
        TG[z] = PS[q, z] + RZ[0, z] + RZ[1, z] + RZ[2, z]
    tg_copy = pltpu.make_async_copy(TG, tg, ls.at[7])
    tg_copy.start()

    for d in range(3):
        xrecv((12 + d,))

        def fn(r):
            for z, p in ((0, 0), (3, 7)):
                put(V.at[0, d, z], r, at(V.at[0, d, z], r) + at(S.at[0, d, p], r) * (SEVENTH * SEVENTH * SEVENTH))

        chunks(fn)
        store(0, d).start()

    xsent(range(15))
    for ph in range(2):
        for k in range(9):
            tcopy(ph, k).wait_send()
    for k in range(4):
        pcopy(k).wait_send()
    for j in range(1, 4):
        zcopy(j).wait_send()
    tg_copy.wait()
    for t in range(2):
        for d in range(3):
            store(t, d).wait()


def body(nslab, template, subject, velocity):
    depth, blk, nx = template.shape
    ny = subject.shape[2]
    tall = ny + 2 * PAD
    vmem = lambda *shape: pltpu.VMEM(shape, F32)
    dma = lambda *shape: pltpu.SemaphoreType.DMA(shape)
    return pl.pallas_call(
        functools.partial(kernel, nslab),
        out_shape=(
            jax.ShapeDtypeStruct(velocity.shape, F32),
            jax.ShapeDtypeStruct(template.shape, F32),
        ),
        in_specs=[pl.BlockSpec(memory_space=pl.ANY)] * 3,
        out_specs=(pl.BlockSpec(memory_space=pl.ANY),) * 2,
        scratch_shapes=[
            vmem(8, tall, nx),
            vmem(6, tall, nx),
            vmem(4, tall, nx),
            vmem(6, tall, nx),
            vmem(2, 3, 8, tall, nx),
            vmem(6, tall, nx),
            vmem(2, 3, 4, tall, nx),
            vmem(2, 3, ny, nx),
            vmem(4, ny, nx),
            vmem(2, ny, nx),
            vmem(2, ny, nx),
            vmem(4, ny, nx),
            vmem(4, 4, blk, nx),
            vmem(4, 4, blk, nx),
            vmem(3, 4, blk, nx),
            vmem(4, blk, nx),
            dma(2, 15), dma(2, 15), dma(2, 9), dma(2, 9), dma(7), dma(7), dma(8),
        ],
        compiler_params=pltpu.CompilerParams(
            collective_id=0, has_side_effects=True, vmem_limit_bytes=56 << 20),
    )(template, subject, velocity)


def solution(mesh):
    return jax.shard_map(
        functools.partial(body, mesh.shape["slab"]),
        mesh=mesh,
        in_specs=(
            P("slab", "subj", None),
            P("subj", "slab", None, None),
            P("subj", None, None, "slab", None, None),
        ),
        out_specs=(P("subj", None, None, "slab", None, None), P("slab", "subj", None)),
        check_vma=False,
    )
```

```python
import functools

import jax
import jax.numpy as jnp
from jax import lax
from jax.experimental import pallas as pl
from jax.experimental.pallas import tpu as pltpu
from jax.sharding import PartitionSpec as P

MESH = pl.DeviceIdType.MESH
F32 = jnp.float32
DT = 0.5
WEIGHT = -2.5
SEVENTH = 1.0 / 7.0
PAD = 8
R = 64


def kernel(
    nslab, tmpl, subj, vel, out, tg,
    T, I1, L2, L1, S, U, V, V0H, SUB, FS, FR, A0, RB, PS, RZ, TG,
    xs, xr, ts, tr, rs, rr, ls,
):
    ny, nx = tmpl.shape[1] * 8, tmpl.shape[2]
    blk = tmpl.shape[1]
    half = blk // 2
    nchunk = ny // R
    g = lax.axis_index("subj")
    s = lax.axis_index("slab")
    q, c = g // 2, lax.rem(g, 2)
    sib = g + 1 - 2 * c
    has_up, has_dn = s < nslab - 1, s > 0

    def ring(k):
        return 2 * lax.rem(q + k, 4) + c

    def rows(b, n=blk):
        return pl.ds(pl.multiple_of(PAD + b, 8), n)

    body = pl.ds(PAD, ny)
    loads = []
    for t in range(2):
        for d in range(3):
            loads.append(pltpu.make_async_copy(vel.at[0, t, d], V.at[t, d, :, body], ls.at[3 * t + d]))
    loads.append(pltpu.make_async_copy(subj.at[0], SUB, ls.at[6]))
    loads.append(pltpu.make_async_copy(tmpl, T.at[pl.ds(0, 4), rows(g * blk)], ls.at[7]))
    for copy in (loads[7], loads[0], loads[1], loads[2], loads[3], loads[4], loads[5], loads[6]):
        copy.start()

    barrier = pltpu.get_barrier_semaphore()

    def greet(**where):
        pl.semaphore_signal(barrier, inc=1, device_id=where, device_id_type=MESH)

    for peer in (sib, ring(1), ring(2), ring(3)):
        greet(subj=peer)

    greet(slab=lax.rem(s + 1, nslab))
    greet(slab=lax.rem(s + nslab - 1, nslab))

    edge = jnp.zeros((PAD, nx), F32)

    def zero_pads(ref, count):
        def step(p, _):
            ref[p, pl.ds(0, PAD)] = edge
            ref[p, pl.ds(PAD + ny, PAD)] = edge
            return 0

        lax.fori_loop(0, count, step, 0)

    zero_pads(T, 8)
    zero_pads(I1, 6)
    zero_pads(L2, 4)
    zero_pads(L1, 6)
    zero_pads(U, 6)
    for t in range(2):
        zero_pads(V.at[t, 1], 4)
        for d in range(3):
            zero_pads(S.at[t, d], 8)

    def zero_plane(ref, first=0):
        def step(i, _):
            ref[pl.ds(pl.multiple_of(first + i * R, 8), R)] = jnp.zeros((R, nx), F32)
            return 0

        lax.fori_loop(0, nchunk, step, 0)

    def zero_side(side):
        planes, seconds, firsts = ((6, 7), 0, 1) if side == 0 else ((4, 5), 7, 6)
        for p in planes:
            for k in range(4):
                T[p, rows((2 * k + c) * blk)] = jnp.zeros((blk, nx), F32)
        for d in range(3):
            zero_plane(V0H.at[side, d])
            zero_plane(S.at[1, d, seconds], PAD)
            zero_plane(S.at[1, d, firsts], PAD)
            zero_plane(S.at[0, d, seconds], PAD)
        zero_plane(FR.at[side])
        zero_plane(L1.at[0 if side == 0 else 5], PAD)
        zero_plane(U.at[0 if side == 0 else 5], PAD)

    @pl.when(s == 0)
    def _():
        zero_side(0)

    @pl.when(s == nslab - 1)
    def _():
        zero_side(1)

    pl.semaphore_wait(barrier, 6)

    def xcopy(k, dirn):
        up = dirn == 0
        if k == 0 or k > 14:
            place = rows((g if k == 0 else ring((3, 1, 2)[k - 15])) * blk)
            src = tmpl.at[pl.ds(2 if up else 0, 2)] if k == 0 else T.at[pl.ds(2 if up else 0, 2), place]
            dst = T.at[pl.ds(6 if up else 4, 2), place]
        elif k < 4:
            src, dst = vel.at[0, 0, k - 1, 3 if up else 0], V0H.at[dirn, k - 1]
        elif k < 7:
            src, dst = S.at[1, k - 4, 4 if up else 3, body], S.at[1, k - 4, 0 if up else 7, body]
        elif k == 7:
            src, dst = FS.at[dirn], FR.at[dirn]
        elif k < 11:
            src, dst = S.at[1, k - 8, 5 if up else 2, body], S.at[1, k - 8, 1 if up else 6, body]
        elif k == 11:
            src, dst = L1.at[4 if up else 1, body], L1.at[0 if up else 5, body]
        else:
            src, dst = S.at[0, k - 12, 4 if up else 3, body], S.at[0, k - 12, 0 if up else 7, body]
        return pltpu.make_async_remote_copy(
            src, dst, xs.at[dirn, k], xr.at[dirn, k],
            device_id={"slab": s + 1 if up else s - 1}, device_id_type=MESH)

    def xstart(ks):
        @pl.when(has_up)
        def _():
            for k in ks:
                xcopy(k, 0).start()

        @pl.when(has_dn)
        def _():
            for k in ks:
                xcopy(k, 1).start()

    def xrecv(ks):
        @pl.when(has_dn)
        def _():
            for k in ks:
                xcopy(k, 0).wait_recv()

        @pl.when(has_up)
        def _():
            for k in ks:
                xcopy(k, 1).wait_recv()

    def xsent(ks):
        @pl.when(has_up)
        def _():
            for k in ks:
                xcopy(k, 0).wait_send()

        @pl.when(has_dn)
        def _():
            for k in ks:
                xcopy(k, 1).wait_send()

    def tcopy(k, recv=False):
        owner = {0: g, 1: g, 2: ring(3), 3: ring(1), 4: g, 5: ring(3), 6: ring(1), 7: ring(2), 8: ring(2)}[k]
        if recv:
            owner = {0: ring(3), 1: ring(1), 2: ring(2), 3: ring(2)}.get(k, owner + 1 - 2 * c)
        off, n = {2: (0, half), 3: (half, half), 7: (0, half), 8: (half, half)}.get(k, (0, blk))
        place = T.at[pl.ds(0, 4), rows(owner * blk + off, n)]
        src = tmpl if k in (0, 1, 4) else place
        peer = {0: ring(1), 1: ring(3), 2: ring(1), 3: ring(3)}.get(k, sib)
        return pltpu.make_async_remote_copy(
            src, place, ts.at[0, k], tr.at[0, k], device_id={"subj": peer}, device_id_type=MESH)

    def hcopy(j, recv=False):
        owner = (g, ring(3), ring(1), ring(2))[j]
        if recv:
            owner = owner + 1 - 2 * c
        place = T.at[pl.ds(4, 4), rows(owner * blk)]
        return pltpu.make_async_remote_copy(
            place, place, ts.at[1, j], tr.at[1, j], device_id={"subj": sib}, device_id_type=MESH)

    def twait(k):
        tcopy(k, True).wait_recv()

    xstart((0,))
    for k in (0, 1, 4):
        tcopy(k).start()
    xstart((1,))
    twait(0)
    tcopy(2).start()
    xstart((15,))
    tcopy(5).start()
    twait(1)
    tcopy(3).start()
    xstart((16, 2))
    tcopy(6).start()
    twait(2)
    tcopy(7).start()
    twait(3)
    xstart((17, 3))
    tcopy(8).start()
    for j, k in enumerate((0, 15, 16, 17)):
        xrecv((k,))
        hcopy(j).start()
    for k in (4, 5, 6, 7, 8):
        twait(k)
    for j in range(4):
        hcopy(j, True).wait_recv()

    lane = lax.broadcasted_iota(jnp.int32, (R, 128), 1)
    first_lane, last_lane = lane == 0, lane == 127

    def left(x):
        y = pltpu.roll(x, 1, 1)
        return jnp.concatenate([jnp.where(first_lane, 0.0, y[:, :128]), y[:, 128:]], axis=1)

    def right(x):
        y = pltpu.roll(x, nx - 1, 1)
        return jnp.concatenate([y[:, : nx - 128], jnp.where(last_lane, 0.0, y[:, nx - 128 :])], axis=1)

    def chunks(fn):
        def step(i, _):
            fn(pl.multiple_of(i * R, R))
            return 0

        lax.fori_loop(0, nchunk, step, 0)

    def at(ref, r):
        return ref[pl.ds(pl.multiple_of(PAD + r, 8), R)]

    def flat(ref, r):
        return ref[pl.ds(r, R)]

    def around(ref, r):
        ext = ref[pl.ds(r, R + 16)]
        n = R + 16
        return ext[8 : 8 + R], pltpu.roll(ext, 1, 0)[8 : 8 + R], pltpu.roll(ext, n - 1, 0)[8 : 8 + R]

    def put(ref, r, x):
        ref[pl.ds(pl.multiple_of(PAD + r, 8), R)] = x

    def advect(plane, below, above, vread, r):
        here, ym, yp = around(plane, r)
        pairs = ((at(below, r), at(above, r)), (ym, yp), (left(here), right(here)))
        diffs, total = [], None
        for d, (minus, plus) in enumerate(pairs):
            v = vread(d, r)
            diff = jnp.where(v >= 0.0, here - minus, plus - here)
            diffs.append(diff)
            total = v * diff if total is None else total + v * diff
        return here - DT * total, diffs

    def forward_0(z):
        if 0 <= z < 4:
            vread = lambda d, r: at(V.at[0, d, z], r)
        else:
            vread = lambda d, r: flat(V0H.at[0 if z < 0 else 1, d], r)

        def fn(r):
            new, diffs = advect(T.at[z % 8], T.at[(z - 1) % 8], T.at[(z + 1) % 8], vread, r)
            put(I1.at[z + 1], r, new)
            for d in range(3):
                put(S.at[0, d, z + 2], r, WEIGHT * diffs[d])

        chunks(fn)

    def forward_1(z):
        def fn(r):
            vread = lambda d, r: at(V.at[1, d, z], r)
            new, diffs = advect(I1.at[z + 1], I1.at[z], I1.at[z + 2], vread, r)
            lam = new - flat(SUB.at[z], r)
            put(L2.at[z], r, lam)
            scaled = WEIGHT * lam
            for d in range(3):
                put(S.at[1, d, z + 2], r, scaled * diffs[d])
            if z == 0:
                FS[1, pl.ds(r, R)] = jnp.maximum(vread(0, r), 0.0) * lam
            if z == 3:
                FS[0, pl.ds(r, R)] = jnp.minimum(vread(0, r), 0.0) * lam

        chunks(fn)

    def backward(t, lam_ref, z, below, above, r):
        lam = at(lam_ref, r)
        vz = at(V.at[t, 0, z], r)
        total = jnp.abs(vz) * lam - above(r) + below(r)
        vy, lam_ext = V[t, 1, z, pl.ds(r, R + 16)], lam_ref[pl.ds(r, R + 16)]
        pos, neg = jnp.maximum(vy, 0.0) * lam_ext, jnp.minimum(vy, 0.0) * lam_ext
        n = R + 16
        total = total + ((pos - neg)[8 : 8 + R] - pltpu.roll(pos, n - 1, 0)[8 : 8 + R] + pltpu.roll(neg, 1, 0)[8 : 8 + R])
        vx = at(V.at[t, 2, z], r)
        pos, neg = jnp.maximum(vx, 0.0) * lam, jnp.minimum(vx, 0.0) * lam
        total = total + ((pos - neg) - right(pos) + left(neg))
        return lam - DT * total

    def backward_1(z):
        def below(r):
            if z == 0:
                return flat(FR.at[0], r)
            return jnp.minimum(at(V.at[1, 0, z - 1], r), 0.0) * at(L2.at[z - 1], r)

        def above(r):
            if z == 3:
                return flat(FR.at[1], r)
            return jnp.maximum(at(V.at[1, 0, z + 1], r), 0.0) * at(L2.at[z + 1], r)

        def fn(r):
            lam = backward(1, L2.at[z], z, below, above, r)
            put(L1.at[z + 1], r, lam)
            for d in range(3):
                put(S.at[0, d, z + 2], r, at(S.at[0, d, z + 2], r) * lam)

        chunks(fn)

    def backward_0(z):
        def below(r):
            v = flat(V0H.at[0, 0], r) if z == 0 else at(V.at[0, 0, z - 1], r)
            return jnp.minimum(v, 0.0) * at(L1.at[z], r)

        def above(r):
            v = flat(V0H.at[1, 0], r) if z == 3 else at(V.at[0, 0, z + 1], r)
            return jnp.maximum(v, 0.0) * at(L1.at[z + 2], r)

        def fn(r):
            A0[z, pl.ds(r, R)] = backward(0, L1.at[z + 1], z, below, above, r)

        chunks(fn)

    def smooth(t, d):
        def sweep(p, low, high, r):
            here, ym, yp = around(S.at[t, d, p], r)
            beside = ym + yp + left(here) + right(here)
            if low:
                beside = beside + at(S.at[t, d, p - 1], r)
            if high:
                beside = beside + at(S.at[t, d, p + 1], r)
            put(U.at[p - 1], r, (here + beside * SEVENTH) * SEVENTH)

        def inner(p, _):
            chunks(lambda r: sweep(p, True, True, r))
            return 0

        lax.fori_loop(2, 6, inner, 0)

        @pl.when(has_dn)
        def _():
            chunks(lambda r: sweep(1, t == 1, True, r))

        @pl.when(has_up)
        def _():
            chunks(lambda r: sweep(6, True, t == 1, r))

        def last(z, _):
            def fn(r):
                here, ym, yp = around(U.at[z + 1], r)
                beside = ym + yp + left(here) + right(here) + at(U.at[z], r) + at(U.at[z + 2], r)
                out[0, t, d, z, pl.ds(r, R)] = at(V.at[t, d, z], r) + (at(S.at[t, d, z + 2], r) + beside) * SEVENTH

            chunks(fn)
            return 0

        lax.fori_loop(0, 4, last, 0)

    for copy in loads:
        copy.wait()
    for z in range(4):
        forward_0(z)
    forward_1(1)
    forward_1(2)
    xstart((4, 5, 6))
    xrecv((1, 2, 3))
    forward_0(-1)
    forward_0(4)
    forward_1(0)
    forward_1(3)
    xstart((7, 8, 9, 10))
    backward_1(1)
    backward_1(2)
    xrecv((7,))
    backward_1(0)
    backward_1(3)
    xstart((11, 12, 13, 14))
    xrecv((4, 5, 6, 8, 9, 10))

    def smooth_1(d, _):
        smooth(1, d)
        return 0

    lax.fori_loop(0, 3, smooth_1, 0)
    xrecv((11,))

    for z in range(4):
        backward_0(z)

    def pcopy(k):
        return pltpu.make_async_remote_copy(
            A0.at[:, pl.ds(pl.multiple_of((2 * k + 1 - c) * blk, 8), blk)], RB.at[k], rs.at[k], rr.at[k],
            device_id={"subj": sib}, device_id_type=MESH)

    for k in range(4):
        pcopy(k).start()

    def scale_halo(p, l):
        def fn(r):
            lam = at(L1.at[l], r)
            for d in range(3):
                put(S.at[0, d, p], r, at(S.at[0, d, p], r) * lam)

        chunks(fn)

    scale_halo(1, 0)
    scale_halo(6, 5)
    for k in range(4):
        pcopy(k).wait_recv()

    def pair_sum(k, _):
        for z in range(4):
            PS[k, z] = A0[z, pl.ds(pl.multiple_of((2 * k + c) * blk, 8), blk)] + RB[k, z]
        return 0

    lax.fori_loop(0, 4, pair_sum, 0)

    def zcopy(j):
        return pltpu.make_async_remote_copy(
            PS.at[lax.rem(q + j, 4)], RZ.at[j - 1], rs.at[3 + j], rr.at[3 + j],
            device_id={"subj": ring(j)}, device_id_type=MESH)

    for j in (2, 1, 3):
        zcopy(j).start()

    def smooth_0(d, _):
        smooth(0, d)
        return 0

    lax.fori_loop(0, 3, smooth_0, 0)
    for j in (1, 3, 2):
        zcopy(j).wait_recv()
    for z in range(4):
        TG[z] = PS[q, z] + RZ[0, z] + RZ[1, z] + RZ[2, z]
    tg_copy = pltpu.make_async_copy(TG, tg, ls.at[7])
    tg_copy.start()

    for d in range(3):
        xrecv((12 + d,))

        def fn(r):
            for z, p in ((0, 0), (3, 7)):
                late = at(S.at[0, d, p], r) * (SEVENTH * SEVENTH * SEVENTH)
                out[0, 0, d, z, pl.ds(r, R)] = out[0, 0, d, z, pl.ds(r, R)] + late

        chunks(fn)

    xsent(range(18))
    for k in range(9):
        tcopy(k).wait_send()
    for j in range(4):
        hcopy(j).wait_send()
    for k in range(4):
        pcopy(k).wait_send()
    for j in range(1, 4):
        zcopy(j).wait_send()
    tg_copy.wait()


def body(nslab, template, subject, velocity):
    depth, blk, nx = template.shape
    ny = subject.shape[2]
    tall = ny + 2 * PAD
    vmem = lambda *shape: pltpu.VMEM(shape, F32)
    dma = lambda *shape: pltpu.SemaphoreType.DMA(shape)
    return pl.pallas_call(
        functools.partial(kernel, nslab),
        out_shape=(
            jax.ShapeDtypeStruct(velocity.shape, F32),
            jax.ShapeDtypeStruct(template.shape, F32),
        ),
        in_specs=[pl.BlockSpec(memory_space=pltpu.HBM)] * 3,
        out_specs=(pl.BlockSpec(memory_space=pltpu.VMEM), pl.BlockSpec(memory_space=pl.ANY)),
        scratch_shapes=[
            vmem(8, tall, nx),
            vmem(6, tall, nx),
            vmem(4, tall, nx),
            vmem(6, tall, nx),
            vmem(2, 3, 8, tall, nx),
            vmem(6, tall, nx),
            vmem(2, 3, 4, tall, nx),
            vmem(2, 3, ny, nx),
            vmem(4, ny, nx),
            vmem(2, ny, nx),
            vmem(2, ny, nx),
            vmem(4, ny, nx),
            vmem(4, 4, blk, nx),
            vmem(4, 4, blk, nx),
            vmem(3, 4, blk, nx),
            vmem(4, blk, nx),
            dma(2, 18), dma(2, 18), dma(2, 9), dma(2, 9), dma(7), dma(7), dma(8),
        ],
        compiler_params=pltpu.CompilerParams(
            collective_id=0, has_side_effects=True, vmem_limit_bytes=40 << 20),
    )(*(pltpu.with_memory_space_constraint(x, pltpu.HBM) for x in (template, subject, velocity)))


def solution(mesh):
    return jax.shard_map(
        functools.partial(body, mesh.shape["slab"]),
        mesh=mesh,
        in_specs=(
            P("slab", "subj", None),
            P("subj", "slab", None, None),
            P("subj", None, None, "slab", None, None),
        ),
        out_specs=(P("subj", None, None, "slab", None, None), P("slab", "subj", None)),
        check_vma=False,
    )
```

```python
import functools

import jax
import jax.numpy as jnp
from jax import lax
from jax.experimental import pallas as pl
from jax.experimental.pallas import tpu as pltpu
from jax.sharding import PartitionSpec as P

MESH = pl.DeviceIdType.MESH
F32 = jnp.float32
DT = 0.5
WEIGHT = -2.5
SEVENTH = 1.0 / 7.0
PAD = 8
R = 64


def kernel(
    nslab, tmpl, subj, vel, out, tg,
    T, I1, L2, L1, S, U, V, V0H, SUB, FS, FR, A0, RB, PS, RH, RZ, TG, GPS, GRH, GRZ, TG2,
    xs, xr, ts, tr, rs, rr, gs, gr, ls,
):
    ny, nx = tmpl.shape[1] * 8, tmpl.shape[2]
    blk = tmpl.shape[1]
    half = blk // 2
    nchunk = ny // R
    g = lax.axis_index("subj")
    s = lax.axis_index("slab")
    q, c = g // 2, lax.rem(g, 2)
    sib = g + 1 - 2 * c
    has_up, has_dn = s < nslab - 1, s > 0

    def ring(k):
        return 2 * lax.rem(q + k, 4) + c

    def rows(b, n=blk):
        return pl.ds(pl.multiple_of(PAD + b, 8), n)

    body = pl.ds(PAD, ny)
    loads = []
    for t in range(2):
        for d in range(3):
            loads.append(pltpu.make_async_copy(vel.at[0, t, d], V.at[t, d, :, body], ls.at[3 * t + d]))
    loads.append(pltpu.make_async_copy(subj.at[0], SUB, ls.at[6]))
    loads.append(pltpu.make_async_copy(tmpl, T.at[pl.ds(0, 4), rows(g * blk)], ls.at[7]))
    for copy in (loads[7], loads[0], loads[1], loads[2], loads[3], loads[4], loads[5], loads[6]):
        copy.start()

    barrier = pltpu.get_barrier_semaphore()

    def greet(**where):
        pl.semaphore_signal(barrier, inc=1, device_id=where, device_id_type=MESH)

    for peer in (sib, ring(1), ring(2), ring(3)):
        greet(subj=peer)

    greet(slab=lax.rem(s + 1, nslab))
    greet(slab=lax.rem(s + nslab - 1, nslab))

    edge = jnp.zeros((PAD, nx), F32)

    def zero_pads(ref, count):
        def step(p, _):
            ref[p, pl.ds(0, PAD)] = edge
            ref[p, pl.ds(PAD + ny, PAD)] = edge
            return 0

        lax.fori_loop(0, count, step, 0)

    zero_pads(T, 8)
    zero_pads(I1, 6)
    zero_pads(L2, 4)
    zero_pads(L1, 6)
    zero_pads(U, 6)
    for t in range(2):
        zero_pads(V.at[t, 1], 4)
        for d in range(3):
            zero_pads(S.at[t, d], 8)

    def zero_plane(ref, first=0):
        def step(i, _):
            ref[pl.ds(pl.multiple_of(first + i * R, 8), R)] = jnp.zeros((R, nx), F32)
            return 0

        lax.fori_loop(0, nchunk, step, 0)

    def zero_side(side):
        planes, seconds, firsts = ((6, 7), 0, 1) if side == 0 else ((4, 5), 7, 6)
        for p in planes:
            for k in range(4):
                T[p, rows((2 * k + c) * blk)] = jnp.zeros((blk, nx), F32)
        for d in range(3):
            zero_plane(V0H.at[side, d])
            zero_plane(S.at[1, d, seconds], PAD)
            zero_plane(S.at[1, d, firsts], PAD)
            zero_plane(S.at[0, d, seconds], PAD)
        zero_plane(FR.at[side])
        zero_plane(L1.at[0 if side == 0 else 5], PAD)
        zero_plane(U.at[0 if side == 0 else 5], PAD)

    @pl.when(s == 0)
    def _():
        zero_side(0)

    @pl.when(s == nslab - 1)
    def _():
        zero_side(1)

    pl.semaphore_wait(barrier, 6)

    def xcopy(k, dirn):
        up = dirn == 0
        if k == 0 or 14 < k < 18:
            place = rows((g if k == 0 else ring((3, 1, 2)[k - 15])) * blk)
            src = tmpl.at[pl.ds(2 if up else 0, 2)] if k == 0 else T.at[pl.ds(2 if up else 0, 2), place]
            dst = T.at[pl.ds(6 if up else 4, 2), place]
        elif k < 4:
            src, dst = vel.at[0, 0, k - 1, 3 if up else 0], V0H.at[dirn, k - 1]
        elif k < 7:
            src, dst = S.at[1, k - 4, 4 if up else 3, body], S.at[1, k - 4, 0 if up else 7, body]
        elif k == 7:
            src, dst = FS.at[dirn], FR.at[dirn]
        elif k < 11:
            src, dst = S.at[1, k - 8, 5 if up else 2, body], S.at[1, k - 8, 1 if up else 6, body]
        elif k == 11:
            src, dst = L1.at[4 if up else 1, body], L1.at[0 if up else 5, body]
        else:
            src, dst = S.at[0, k - 12, 4 if up else 3, body], S.at[0, k - 12, 0 if up else 7, body]
        return pltpu.make_async_remote_copy(
            src, dst, xs.at[dirn, k], xr.at[dirn, k],
            device_id={"slab": s + 1 if up else s - 1}, device_id_type=MESH)

    def xeach(ks, up, dn, fn):
        @pl.when(up)
        def _():
            for k in ks:
                fn(xcopy(k, 0))

        @pl.when(dn)
        def _():
            for k in ks:
                fn(xcopy(k, 1))

    def xstart(ks, up=has_up, dn=has_dn):
        xeach(ks, up, dn, lambda copy: copy.start())

    def xrecv(ks):
        @pl.when(has_dn)
        def _():
            for k in ks:
                xcopy(k, 0).wait_recv()

        @pl.when(has_up)
        def _():
            for k in ks:
                xcopy(k, 1).wait_recv()

    def xsent(ks, up=has_up, dn=has_dn):
        xeach(ks, up, dn, lambda copy: copy.wait_send())

    def tcopy(k, recv=False):
        owner = {0: g, 1: g, 2: ring(3), 3: ring(1), 4: g, 5: ring(3), 6: ring(1), 7: ring(2), 8: ring(2)}[k]
        if recv:
            owner = {0: ring(3), 1: ring(1), 2: ring(2), 3: ring(2)}.get(k, owner + 1 - 2 * c)
        off, n = {2: (0, half), 3: (half, half), 7: (0, half), 8: (half, half)}.get(k, (0, blk))
        place = T.at[pl.ds(0, 4), rows(owner * blk + off, n)]
        src = tmpl if k in (0, 1, 4) else place
        peer = {0: ring(1), 1: ring(3), 2: ring(1), 3: ring(3)}.get(k, sib)
        return pltpu.make_async_remote_copy(
            src, place, ts.at[0, k], tr.at[0, k], device_id={"subj": peer}, device_id_type=MESH)

    def hcopy(j, recv=False):
        owner = (g, ring(3), ring(1), ring(2))[j]
        if recv:
            owner = owner + 1 - 2 * c
        place = T.at[pl.ds(4, 4), rows(owner * blk)]
        return pltpu.make_async_remote_copy(
            place, place, ts.at[1, j], tr.at[1, j], device_id={"subj": sib}, device_id_type=MESH)

    def twait(k):
        tcopy(k, True).wait_recv()

    cross_up, cross_dn = has_up & (lax.rem(s, 4) == 3), has_dn & (lax.rem(s, 4) == 0)
    near_up, near_dn = has_up & (lax.rem(s, 4) != 3), has_dn & (lax.rem(s, 4) != 0)

    xstart((0,))
    for k in (0, 1, 4):
        tcopy(k).start()
    xstart((1,), near_up, near_dn)
    twait(0)
    tcopy(2).start()
    xstart((15,))
    tcopy(5).start()
    twait(1)
    tcopy(3).start()
    xstart((16,))
    xstart((2,), near_up, near_dn)
    tcopy(6).start()
    twait(2)
    tcopy(7).start()
    twait(3)
    xstart((17,))
    xstart((3,), near_up, near_dn)
    xstart((1, 2, 3), cross_up, cross_dn)
    tcopy(8).start()
    for j, k in enumerate((0, 15, 16, 17)):
        xrecv((k,))
        hcopy(j).start()
    for k in (4, 5, 6, 7, 8):
        twait(k)
    for j in range(4):
        hcopy(j, True).wait_recv()

    lane = lax.broadcasted_iota(jnp.int32, (R, 128), 1)
    first_lane, last_lane = lane == 0, lane == 127

    def left(x):
        y = pltpu.roll(x, 1, 1)
        return jnp.concatenate([jnp.where(first_lane, 0.0, y[:, :128]), y[:, 128:]], axis=1)

    def right(x):
        y = pltpu.roll(x, nx - 1, 1)
        return jnp.concatenate([y[:, : nx - 128], jnp.where(last_lane, 0.0, y[:, nx - 128 :])], axis=1)

    def chunks(fn):
        def step(i, _):
            fn(pl.multiple_of(i * R, R))
            return 0

        lax.fori_loop(0, nchunk, step, 0)

    def at(ref, r):
        return ref[pl.ds(pl.multiple_of(PAD + r, 8), R)]

    def flat(ref, r):
        return ref[pl.ds(r, R)]

    def around(ref, r):
        ext = ref[pl.ds(r, R + 16)]
        n = R + 16
        return ext[8 : 8 + R], pltpu.roll(ext, 1, 0)[8 : 8 + R], pltpu.roll(ext, n - 1, 0)[8 : 8 + R]

    def put(ref, r, x):
        ref[pl.ds(pl.multiple_of(PAD + r, 8), R)] = x

    def advect(plane, below, above, vread, r):
        here, ym, yp = around(plane, r)
        pairs = ((at(below, r), at(above, r)), (ym, yp), (left(here), right(here)))
        diffs, total = [], None
        for d, (minus, plus) in enumerate(pairs):
            v = vread(d, r)
            diff = jnp.where(v >= 0.0, here - minus, plus - here)
            diffs.append(diff)
            total = v * diff if total is None else total + v * diff
        return here - DT * total, diffs

    def forward_0(z):
        if 0 <= z < 4:
            vread = lambda d, r: at(V.at[0, d, z], r)
        else:
            vread = lambda d, r: flat(V0H.at[0 if z < 0 else 1, d], r)

        def fn(r):
            new, diffs = advect(T.at[z % 8], T.at[(z - 1) % 8], T.at[(z + 1) % 8], vread, r)
            put(I1.at[z + 1], r, new)
            for d in range(3):
                put(S.at[0, d, z + 2], r, WEIGHT * diffs[d])

        chunks(fn)

    def forward_1(z):
        def fn(r):
            vread = lambda d, r: at(V.at[1, d, z], r)
            new, diffs = advect(I1.at[z + 1], I1.at[z], I1.at[z + 2], vread, r)
            lam = new - flat(SUB.at[z], r)
            put(L2.at[z], r, lam)
            scaled = WEIGHT * lam
            for d in range(3):
                put(S.at[1, d, z + 2], r, scaled * diffs[d])
            if z == 0:
                FS[1, pl.ds(r, R)] = jnp.maximum(vread(0, r), 0.0) * lam
            if z == 3:
                FS[0, pl.ds(r, R)] = jnp.minimum(vread(0, r), 0.0) * lam

        chunks(fn)

    def backward(t, lam_ref, z, below, above, r):
        lam = at(lam_ref, r)
        vz = at(V.at[t, 0, z], r)
        total = jnp.abs(vz) * lam - above(r) + below(r)
        vy, lam_ext = V[t, 1, z, pl.ds(r, R + 16)], lam_ref[pl.ds(r, R + 16)]
        pos, neg = jnp.maximum(vy, 0.0) * lam_ext, jnp.minimum(vy, 0.0) * lam_ext
        n = R + 16
        total = total + ((pos - neg)[8 : 8 + R] - pltpu.roll(pos, n - 1, 0)[8 : 8 + R] + pltpu.roll(neg, 1, 0)[8 : 8 + R])
        vx = at(V.at[t, 2, z], r)
        pos, neg = jnp.maximum(vx, 0.0) * lam, jnp.minimum(vx, 0.0) * lam
        total = total + ((pos - neg) - right(pos) + left(neg))
        return lam - DT * total

    def backward_1(z):
        def below(r):
            if z == 0:
                return flat(FR.at[0], r)
            return jnp.minimum(at(V.at[1, 0, z - 1], r), 0.0) * at(L2.at[z - 1], r)

        def above(r):
            if z == 3:
                return flat(FR.at[1], r)
            return jnp.maximum(at(V.at[1, 0, z + 1], r), 0.0) * at(L2.at[z + 1], r)

        def fn(r):
            lam = backward(1, L2.at[z], z, below, above, r)
            put(L1.at[z + 1], r, lam)
            for d in range(3):
                put(S.at[0, d, z + 2], r, at(S.at[0, d, z + 2], r) * lam)

        chunks(fn)

    def backward_0(z):
        def below(r):
            v = flat(V0H.at[0, 0], r) if z == 0 else at(V.at[0, 0, z - 1], r)
            return jnp.minimum(v, 0.0) * at(L1.at[z], r)

        def above(r):
            v = flat(V0H.at[1, 0], r) if z == 3 else at(V.at[0, 0, z + 1], r)
            return jnp.maximum(v, 0.0) * at(L1.at[z + 2], r)

        def fn(r):
            A0[z, pl.ds(r, R)] = backward(0, L1.at[z + 1], z, below, above, r)

        chunks(fn)

    def smooth(t, d):
        def sweep(p, low, high, r):
            here, ym, yp = around(S.at[t, d, p], r)
            beside = ym + yp + left(here) + right(here)
            if low:
                beside = beside + at(S.at[t, d, p - 1], r)
            if high:
                beside = beside + at(S.at[t, d, p + 1], r)
            put(U.at[p - 1], r, (here + beside * SEVENTH) * SEVENTH)

        def inner(p, _):
            chunks(lambda r: sweep(p, True, True, r))
            return 0

        lax.fori_loop(2, 6, inner, 0)

        @pl.when(has_dn)
        def _():
            chunks(lambda r: sweep(1, t == 1, True, r))

        @pl.when(has_up)
        def _():
            chunks(lambda r: sweep(6, True, t == 1, r))

        def last(z, _):
            def fn(r):
                here, ym, yp = around(U.at[z + 1], r)
                beside = ym + yp + left(here) + right(here) + at(U.at[z], r) + at(U.at[z + 2], r)
                out[0, t, d, z, pl.ds(r, R)] = at(V.at[t, d, z], r) + (at(S.at[t, d, z + 2], r) + beside) * SEVENTH

            chunks(fn)
            return 0

        lax.fori_loop(0, 4, last, 0)

    for copy in loads:
        copy.wait()
    for z in range(4):
        forward_0(z)
    forward_1(1)
    forward_1(2)
    xstart((4, 5))
    xrecv((1, 2, 3))
    forward_0(-1)
    forward_0(4)
    forward_1(0)
    forward_1(3)
    xstart((7,))
    backward_1(1)
    backward_1(2)
    xsent((4,))
    xstart((6,))
    xrecv((7,))
    backward_1(0)
    backward_1(3)
    xstart((11,))
    xsent((5,))
    xstart((8,))
    xsent((6,))
    xstart((9,))
    xrecv((11,))

    for z in range(4):
        backward_0(z)

    def pcopy(k):
        return pltpu.make_async_remote_copy(
            A0.at[:, pl.ds(pl.multiple_of((2 * k + 1 - c) * blk, 8), blk)], RB.at[k], rs.at[k], rr.at[k],
            device_id={"subj": sib}, device_id_type=MESH)

    for k in range(4):
        pcopy(k).start()

    def scale_halo(p, l):
        def fn(r):
            lam = at(L1.at[l], r)
            for d in range(3):
                put(S.at[0, d, p], r, at(S.at[0, d, p], r) * lam)

        chunks(fn)

    scale_halo(1, 0)
    scale_halo(6, 5)
    for k in range(4):
        pcopy(k).wait_recv()

    def pair_sum(k, _):
        for z in range(4):
            PS[k, z] = A0[z, pl.ds(pl.multiple_of((2 * k + c) * blk, 8), blk)] + RB[k, z]
        return 0

    lax.fori_loop(0, 4, pair_sum, 0)

    turn = lax.rem(s, 4)
    is_host = (turn == 1) | (turn == 2)
    is_guest = (turn == 0) | (turn == 3)
    partner = s + 1 - 2 * lax.rem(turn, 2)

    def gcopy(j):
        return pltpu.make_async_remote_copy(
            PS.at[lax.rem(q + j, 4)], GPS.at[lax.rem(q + j, 4)], gs.at[j], gr.at[j],
            device_id={"slab": partner}, device_id_type=MESH)

    def give_back():
        return pltpu.make_async_remote_copy(
            TG2, RZ.at[0], gs.at[0], gr.at[0], device_id={"slab": partner}, device_id_type=MESH)

    def hsum(j, o):
        return pltpu.make_async_remote_copy(
            (PS, GPS)[o].at[lax.rem(q + 2, 4), :, pl.ds(half * j, half)], (RH, GRH)[o].at[j],
            rs.at[4 + 4 * o + j], rr.at[4 + 4 * o + j], device_id={"subj": ring((1, 3)[j])}, device_id_type=MESH)

    def zcopy(j, o):
        return pltpu.make_async_remote_copy(
            (PS, GPS)[o].at[lax.rem(q + (1, 3)[j], 4)], (RZ, GRZ)[o].at[j],
            rs.at[6 + 4 * o + j], rr.at[6 + 4 * o + j], device_id={"subj": ring((1, 3)[j])}, device_id_type=MESH)

    def ring_start(o):
        for j in range(2):
            hsum(j, o).start()

    def ring_next(o):
        ref, got = (PS, GPS)[o], (RH, GRH)[o]
        for j in range(2):
            hsum(j, o).wait_recv()
            k = lax.rem(q + (1, 3)[j], 4)
            for z in range(4):
                ref[k, z, pl.ds(half * j, half)] = ref[k, z, pl.ds(half * j, half)] + got[j, z]
            zcopy(j, o).start()

    held_up, held_dn = has_up & (turn == 0), has_dn & (turn == 3)
    free_up, free_dn = has_up & (turn != 0), has_dn & (turn != 3)

    @pl.when(is_guest)
    def _():
        for j in (2, 1, 3):
            gcopy(j).start()

    @pl.when(is_host)
    def _():
        ring_start(0)

    xstart((10, 12, 13, 14), free_up, free_dn)
    smooth(0, 0)

    @pl.when(is_host)
    def _():
        ring_next(0)
        gcopy(2).wait_recv()
        ring_start(1)

    xsent((8,), held_up, held_dn)
    xstart((10,), held_up, held_dn)
    smooth(0, 1)

    @pl.when(is_host)
    def _():
        gcopy(1).wait_recv()
        gcopy(3).wait_recv()
        ring_next(1)

    xstart((12,), held_up, held_dn)
    smooth(0, 2)
    xstart((13, 14), held_up, held_dn)

    @pl.when(is_host)
    def _():
        for o in range(2):
            for j in range(2):
                zcopy(j, o).wait_recv()
        for z in range(4):
            TG2[z] = GRZ[0, z] + GRZ[1, z]
        give_back().start()
        for z in range(4):
            TG[z] = PS[q, z] + RZ[0, z] + RZ[1, z]

    xrecv((4, 5, 6, 8, 9, 10))

    def smooth_1(d, _):
        smooth(1, d)
        return 0

    lax.fori_loop(0, 3, smooth_1, 0)

    @pl.when(is_guest)
    def _():
        give_back().wait_recv()
        for z in range(4):
            TG[z] = PS[q, z] + RZ[0, z]

    tg_copy = pltpu.make_async_copy(TG, tg, ls.at[7])
    tg_copy.start()

    for d in range(3):
        xrecv((12 + d,))

        def fn(r):
            for z, p in ((0, 0), (3, 7)):
                late = at(S.at[0, d, p], r) * (SEVENTH * SEVENTH * SEVENTH)
                out[0, 0, d, z, pl.ds(r, R)] = out[0, 0, d, z, pl.ds(r, R)] + late

        chunks(fn)

    xsent((0, 1, 2, 3, 7, 9, 10, 11, 12, 13, 14, 15, 16, 17))
    xsent((8,), free_up, free_dn)
    for k in range(9):
        tcopy(k).wait_send()
    for j in range(4):
        hcopy(j).wait_send()
    for k in range(4):
        pcopy(k).wait_send()

    @pl.when(is_host)
    def _():
        for o in range(2):
            for j in range(2):
                hsum(j, o).wait_send()
                zcopy(j, o).wait_send()
        give_back().wait_send()

    @pl.when(is_guest)
    def _():
        for j in range(1, 4):
            gcopy(j).wait_send()

    tg_copy.wait()


def body(nslab, template, subject, velocity):
    depth, blk, nx = template.shape
    ny = subject.shape[2]
    tall = ny + 2 * PAD
    vmem = lambda *shape: pltpu.VMEM(shape, F32)
    dma = lambda *shape: pltpu.SemaphoreType.DMA(shape)
    return pl.pallas_call(
        functools.partial(kernel, nslab),
        out_shape=(
            jax.ShapeDtypeStruct(velocity.shape, F32),
            jax.ShapeDtypeStruct(template.shape, F32),
        ),
        in_specs=[pl.BlockSpec(memory_space=pltpu.HBM)] * 3,
        out_specs=(pl.BlockSpec(memory_space=pltpu.VMEM), pl.BlockSpec(memory_space=pl.ANY)),
        scratch_shapes=[
            vmem(8, tall, nx),
            vmem(6, tall, nx),
            vmem(4, tall, nx),
            vmem(6, tall, nx),
            vmem(2, 3, 8, tall, nx),
            vmem(6, tall, nx),
            vmem(2, 3, 4, tall, nx),
            vmem(2, 3, ny, nx),
            vmem(4, ny, nx),
            vmem(2, ny, nx),
            vmem(2, ny, nx),
            vmem(4, ny, nx),
            vmem(4, 4, blk, nx),
            vmem(4, 4, blk, nx),
            vmem(2, 4, blk // 2, nx),
            vmem(2, 4, blk, nx),
            vmem(4, blk, nx),
            vmem(4, 4, blk, nx),
            vmem(2, 4, blk // 2, nx),
            vmem(2, 4, blk, nx),
            vmem(4, blk, nx),
            dma(2, 18), dma(2, 18), dma(2, 9), dma(2, 9), dma(12), dma(12), dma(4), dma(4), dma(8),
        ],
        compiler_params=pltpu.CompilerParams(
            collective_id=0, has_side_effects=True, vmem_limit_bytes=40 << 20),
    )(*(pltpu.with_memory_space_constraint(x, pltpu.HBM) for x in (template, subject, velocity)))


def solution(mesh):
    return jax.shard_map(
        functools.partial(body, mesh.shape["slab"]),
        mesh=mesh,
        in_specs=(
            P("slab", "subj", None),
            P("subj", "slab", None, None),
            P("subj", None, None, "slab", None, None),
        ),
        out_specs=(P("subj", None, None, "slab", None, None), P("slab", "subj", None)),
        check_vma=False,
    )
```

```python
import functools

import jax
import jax.numpy as jnp
from jax import lax
from jax.experimental import pallas as pl
from jax.experimental.pallas import tpu as pltpu
from jax.sharding import PartitionSpec as P

MESH = pl.DeviceIdType.MESH
F32 = jnp.float32
DT = 0.5
WEIGHT = -2.5
SEVENTH = 1.0 / 7.0
PAD = 8
R = 64


def kernel(
    nslab, tmpl, subj, vel, out, tg,
    T, I1, L2, L1, S, U, V, V0H, SUB, FS, FR, A0, RB, PS, RH, RZ, TG, GPS, GRH, GRZ, TG2,
    xs, xr, ts, tr, rs, rr, gs, gr, ls,
):
    ny, nx = tmpl.shape[1] * 8, tmpl.shape[2]
    blk = tmpl.shape[1]
    half = blk // 2
    nchunk = ny // R
    g = lax.axis_index("subj")
    s = lax.axis_index("slab")
    q, c = g // 2, lax.rem(g, 2)
    sib = g + 1 - 2 * c
    has_up, has_dn = s < nslab - 1, s > 0

    def ring(k):
        return 2 * lax.rem(q + k, 4) + c

    def rows(b, n=blk):
        return pl.ds(pl.multiple_of(PAD + b, 8), n)

    body = pl.ds(PAD, ny)
    loads = []
    for t in range(2):
        for d in range(3):
            loads.append(pltpu.make_async_copy(vel.at[0, t, d], V.at[t, d, :, body], ls.at[3 * t + d]))
    loads.append(pltpu.make_async_copy(subj.at[0], SUB, ls.at[6]))
    loads.append(pltpu.make_async_copy(tmpl, T.at[pl.ds(0, 4), rows(g * blk)], ls.at[7]))
    for copy in (loads[7], loads[0], loads[1], loads[2], loads[3], loads[4], loads[5], loads[6]):
        copy.start()

    barrier = pltpu.get_barrier_semaphore()

    def greet(**where):
        pl.semaphore_signal(barrier, inc=1, device_id=where, device_id_type=MESH)

    for peer in (sib, ring(1), ring(2), ring(3)):
        greet(subj=peer)

    greet(slab=lax.rem(s + 1, nslab))
    greet(slab=lax.rem(s + nslab - 1, nslab))

    edge = jnp.zeros((PAD, nx), F32)

    def zero_pads(ref, count):
        def step(p, _):
            ref[p, pl.ds(0, PAD)] = edge
            ref[p, pl.ds(PAD + ny, PAD)] = edge
            return 0

        lax.fori_loop(0, count, step, 0)

    zero_pads(T, 8)
    zero_pads(I1, 6)
    zero_pads(L2, 4)
    zero_pads(L1, 6)
    zero_pads(U, 6)
    for t in range(2):
        zero_pads(V.at[t, 1], 4)
        for d in range(3):
            zero_pads(S.at[t, d], 8)

    def zero_plane(ref, first=0):
        def step(i, _):
            ref[pl.ds(pl.multiple_of(first + i * R, 8), R)] = jnp.zeros((R, nx), F32)
            return 0

        lax.fori_loop(0, nchunk, step, 0)

    def zero_side(side):
        planes, seconds, firsts = ((6, 7), 0, 1) if side == 0 else ((4, 5), 7, 6)
        for p in planes:
            for k in range(4):
                T[p, rows((2 * k + c) * blk)] = jnp.zeros((blk, nx), F32)
        for d in range(3):
            zero_plane(V0H.at[side, d])
            zero_plane(S.at[1, d, seconds], PAD)
            zero_plane(S.at[1, d, firsts], PAD)
            zero_plane(S.at[0, d, seconds], PAD)
        zero_plane(FR.at[side])
        zero_plane(L1.at[0 if side == 0 else 5], PAD)
        zero_plane(U.at[0 if side == 0 else 5], PAD)

    @pl.when(s == 0)
    def _():
        zero_side(0)

    @pl.when(s == nslab - 1)
    def _():
        zero_side(1)

    pl.semaphore_wait(barrier, 6)

    def xcopy(k, dirn):
        up = dirn == 0
        if k == 0 or 14 < k < 18:
            place = rows((g if k == 0 else ring((3, 1, 2)[k - 15])) * blk)
            src = tmpl.at[pl.ds(2 if up else 0, 2)] if k == 0 else T.at[pl.ds(2 if up else 0, 2), place]
            dst = T.at[pl.ds(6 if up else 4, 2), place]
        elif k < 4:
            src, dst = vel.at[0, 0, k - 1, 3 if up else 0], V0H.at[dirn, k - 1]
        elif k < 7:
            src, dst = S.at[1, k - 4, 4 if up else 3, body], S.at[1, k - 4, 0 if up else 7, body]
        elif k == 7:
            src, dst = FS.at[dirn], FR.at[dirn]
        elif k < 11:
            src, dst = S.at[1, k - 8, 5 if up else 2, body], S.at[1, k - 8, 1 if up else 6, body]
        elif k == 11:
            src, dst = L1.at[4 if up else 1, body], L1.at[0 if up else 5, body]
        else:
            src, dst = S.at[0, k - 12, 4 if up else 3, body], S.at[0, k - 12, 0 if up else 7, body]
        return pltpu.make_async_remote_copy(
            src, dst, xs.at[dirn, k], xr.at[dirn, k],
            device_id={"slab": s + 1 if up else s - 1}, device_id_type=MESH)

    def xeach(ks, up, dn, fn):
        @pl.when(up)
        def _():
            for k in ks:
                fn(xcopy(k, 0))

        @pl.when(dn)
        def _():
            for k in ks:
                fn(xcopy(k, 1))

    def xstart(ks, up=has_up, dn=has_dn):
        xeach(ks, up, dn, lambda copy: copy.start())

    def xrecv(ks):
        @pl.when(has_dn)
        def _():
            for k in ks:
                xcopy(k, 0).wait_recv()

        @pl.when(has_up)
        def _():
            for k in ks:
                xcopy(k, 1).wait_recv()

    def xsent(ks, up=has_up, dn=has_dn):
        xeach(ks, up, dn, lambda copy: copy.wait_send())

    def tcopy(k, recv=False):
        owner = {0: g, 1: g, 2: ring(3), 3: ring(1), 4: g, 5: ring(3), 6: ring(1), 7: ring(2), 8: ring(2)}[k]
        if recv:
            owner = {0: ring(3), 1: ring(1), 2: ring(2), 3: ring(2)}.get(k, owner + 1 - 2 * c)
        off, n = {2: (0, half), 3: (half, half), 7: (0, half), 8: (half, half)}.get(k, (0, blk))
        place = T.at[pl.ds(0, 4), rows(owner * blk + off, n)]
        src = tmpl if k in (0, 1, 4) else place
        peer = {0: ring(1), 1: ring(3), 2: ring(1), 3: ring(3)}.get(k, sib)
        return pltpu.make_async_remote_copy(
            src, place, ts.at[0, k], tr.at[0, k], device_id={"subj": peer}, device_id_type=MESH)

    def hcopy(j, recv=False):
        owner = (g, ring(3), ring(1), ring(2))[j]
        if recv:
            owner = owner + 1 - 2 * c
        place = T.at[pl.ds(4, 4), rows(owner * blk)]
        return pltpu.make_async_remote_copy(
            place, place, ts.at[1, j], tr.at[1, j], device_id={"subj": sib}, device_id_type=MESH)

    def twait(k):
        tcopy(k, True).wait_recv()

    cross_up, cross_dn = has_up & (lax.rem(s, 4) == 3), has_dn & (lax.rem(s, 4) == 0)
    near_up, near_dn = has_up & (lax.rem(s, 4) != 3), has_dn & (lax.rem(s, 4) != 0)

    xstart((0,))
    for k in (0, 1, 4):
        tcopy(k).start()
    xstart((1,), near_up, near_dn)
    twait(0)
    tcopy(2).start()
    xstart((15,))
    tcopy(5).start()
    twait(1)
    tcopy(3).start()
    xstart((16,))
    xstart((2,), near_up, near_dn)
    tcopy(6).start()
    twait(2)
    tcopy(7).start()
    twait(3)
    xstart((17,))
    xstart((3,), near_up, near_dn)
    xstart((1, 2, 3), cross_up, cross_dn)
    tcopy(8).start()
    for j, k in enumerate((0, 15, 16, 17)):
        xrecv((k,))
        hcopy(j).start()
    for k in (4, 5, 6, 7, 8):
        twait(k)
    for j in range(4):
        hcopy(j, True).wait_recv()

    lane = lax.broadcasted_iota(jnp.int32, (R, 128), 1)
    first_lane, last_lane = lane == 0, lane == 127

    def left(x):
        y = pltpu.roll(x, 1, 1)
        return jnp.concatenate([jnp.where(first_lane, 0.0, y[:, :128]), y[:, 128:]], axis=1)

    def right(x):
        y = pltpu.roll(x, nx - 1, 1)
        return jnp.concatenate([y[:, : nx - 128], jnp.where(last_lane, 0.0, y[:, nx - 128 :])], axis=1)

    def chunks(fn):
        def step(i, _):
            fn(pl.multiple_of(i * R, R))
            return 0

        lax.fori_loop(0, nchunk, step, 0)

    def at(ref, r):
        return ref[pl.ds(pl.multiple_of(PAD + r, 8), R)]

    def flat(ref, r):
        return ref[pl.ds(r, R)]

    def around(ref, r):
        ext = ref[pl.ds(r, R + 16)]
        n = R + 16
        return ext[8 : 8 + R], pltpu.roll(ext, 1, 0)[8 : 8 + R], pltpu.roll(ext, n - 1, 0)[8 : 8 + R]

    def put(ref, r, x):
        ref[pl.ds(pl.multiple_of(PAD + r, 8), R)] = x

    def advect(plane, below, above, vread, r):
        here, ym, yp = around(plane, r)
        pairs = ((at(below, r), at(above, r)), (ym, yp), (left(here), right(here)))
        diffs, total = [], None
        for d, (minus, plus) in enumerate(pairs):
            v = vread(d, r)
            diff = jnp.where(v >= 0.0, here - minus, plus - here)
            diffs.append(diff)
            total = v * diff if total is None else total + v * diff
        return here - DT * total, diffs

    def forward_0(z):
        if 0 <= z < 4:
            vread = lambda d, r: at(V.at[0, d, z], r)
        else:
            vread = lambda d, r: flat(V0H.at[0 if z < 0 else 1, d], r)

        def fn(r):
            new, diffs = advect(T.at[z % 8], T.at[(z - 1) % 8], T.at[(z + 1) % 8], vread, r)
            put(I1.at[z + 1], r, new)
            for d in range(3):
                put(S.at[0, d, z + 2], r, WEIGHT * diffs[d])

        chunks(fn)

    def forward_1(z):
        def fn(r):
            vread = lambda d, r: at(V.at[1, d, z], r)
            new, diffs = advect(I1.at[z + 1], I1.at[z], I1.at[z + 2], vread, r)
            lam = new - flat(SUB.at[z], r)
            put(L2.at[z], r, lam)
            scaled = WEIGHT * lam
            for d in range(3):
                put(S.at[1, d, z + 2], r, scaled * diffs[d])
            if z == 0:
                FS[1, pl.ds(r, R)] = jnp.maximum(vread(0, r), 0.0) * lam
            if z == 3:
                FS[0, pl.ds(r, R)] = jnp.minimum(vread(0, r), 0.0) * lam

        chunks(fn)

    def backward(t, lam_ref, z, below, above, r):
        lam = at(lam_ref, r)
        vz = at(V.at[t, 0, z], r)
        total = jnp.abs(vz) * lam - above(r) + below(r)
        vy, lam_ext = V[t, 1, z, pl.ds(r, R + 16)], lam_ref[pl.ds(r, R + 16)]
        pos, neg = jnp.maximum(vy, 0.0) * lam_ext, jnp.minimum(vy, 0.0) * lam_ext
        n = R + 16
        total = total + ((pos - neg)[8 : 8 + R] - pltpu.roll(pos, n - 1, 0)[8 : 8 + R] + pltpu.roll(neg, 1, 0)[8 : 8 + R])
        vx = at(V.at[t, 2, z], r)
        pos, neg = jnp.maximum(vx, 0.0) * lam, jnp.minimum(vx, 0.0) * lam
        total = total + ((pos - neg) - right(pos) + left(neg))
        return lam - DT * total

    def backward_1(z):
        def below(r):
            if z == 0:
                return flat(FR.at[0], r)
            return jnp.minimum(at(V.at[1, 0, z - 1], r), 0.0) * at(L2.at[z - 1], r)

        def above(r):
            if z == 3:
                return flat(FR.at[1], r)
            return jnp.maximum(at(V.at[1, 0, z + 1], r), 0.0) * at(L2.at[z + 1], r)

        def fn(r):
            lam = backward(1, L2.at[z], z, below, above, r)
            put(L1.at[z + 1], r, lam)
            for d in range(3):
                put(S.at[0, d, z + 2], r, at(S.at[0, d, z + 2], r) * lam)

        chunks(fn)

    def backward_0(z):
        def below(r):
            v = flat(V0H.at[0, 0], r) if z == 0 else at(V.at[0, 0, z - 1], r)
            return jnp.minimum(v, 0.0) * at(L1.at[z], r)

        def above(r):
            v = flat(V0H.at[1, 0], r) if z == 3 else at(V.at[0, 0, z + 1], r)
            return jnp.maximum(v, 0.0) * at(L1.at[z + 2], r)

        def fn(r):
            A0[z, pl.ds(r, R)] = backward(0, L1.at[z + 1], z, below, above, r)

        chunks(fn)

    def smooth(t, d):
        def sweep(p, low, high, r):
            here, ym, yp = around(S.at[t, d, p], r)
            beside = ym + yp + left(here) + right(here)
            if low:
                beside = beside + at(S.at[t, d, p - 1], r)
            if high:
                beside = beside + at(S.at[t, d, p + 1], r)
            put(U.at[p - 1], r, (here + beside * SEVENTH) * SEVENTH)

        def inner(p, _):
            chunks(lambda r: sweep(p, True, True, r))
            return 0

        lax.fori_loop(2, 6, inner, 0)

        @pl.when(has_dn)
        def _():
            chunks(lambda r: sweep(1, t == 1, True, r))

        @pl.when(has_up)
        def _():
            chunks(lambda r: sweep(6, True, t == 1, r))

        def last(z, _):
            def fn(r):
                here, ym, yp = around(U.at[z + 1], r)
                beside = ym + yp + left(here) + right(here) + at(U.at[z], r) + at(U.at[z + 2], r)
                out[0, t, d, z, pl.ds(r, R)] = at(V.at[t, d, z], r) + (at(S.at[t, d, z + 2], r) + beside) * SEVENTH

            chunks(fn)
            return 0

        lax.fori_loop(0, 4, last, 0)

    for copy in loads:
        copy.wait()
    for z in range(4):
        forward_0(z)
    forward_1(1)
    forward_1(2)
    xstart((4, 5))
    xrecv((1, 2, 3))
    forward_0(-1)
    forward_0(4)
    forward_1(0)
    forward_1(3)
    xstart((7,))
    backward_1(1)
    backward_1(2)
    xsent((4,))
    xstart((6,))
    xrecv((7,))
    backward_1(0)
    backward_1(3)
    xstart((11,))
    xsent((5,))
    xstart((8,))
    xsent((6,))
    xstart((9,))
    xrecv((11,))

    for z in range(4):
        backward_0(z)

    def pcopy(k):
        return pltpu.make_async_remote_copy(
            A0.at[:, pl.ds(pl.multiple_of((2 * k + 1 - c) * blk, 8), blk)], RB.at[k], rs.at[k], rr.at[k],
            device_id={"subj": sib}, device_id_type=MESH)

    for k in range(4):
        pcopy(k).start()

    def scale_halo(p, l):
        def fn(r):
            lam = at(L1.at[l], r)
            for d in range(3):
                put(S.at[0, d, p], r, at(S.at[0, d, p], r) * lam)

        chunks(fn)

    scale_halo(1, 0)
    scale_halo(6, 5)
    for k in range(4):
        pcopy(k).wait_recv()

    def pair_sum(k, _):
        for z in range(4):
            PS[k, z] = A0[z, pl.ds(pl.multiple_of((2 * k + c) * blk, 8), blk)] + RB[k, z]
        return 0

    lax.fori_loop(0, 4, pair_sum, 0)

    turn = lax.rem(s, 4)
    is_host = (turn == 1) | (turn == 2)
    is_guest = (turn == 0) | (turn == 3)
    partner = s + 1 - 2 * lax.rem(turn, 2)

    def gcopy(j):
        return pltpu.make_async_remote_copy(
            PS.at[lax.rem(q + j, 4)], GPS.at[lax.rem(q + j, 4)], gs.at[j], gr.at[j],
            device_id={"slab": partner}, device_id_type=MESH)

    def give_back():
        return pltpu.make_async_remote_copy(
            TG2, RZ.at[0], gs.at[0], gr.at[0], device_id={"slab": partner}, device_id_type=MESH)

    def hsum(j, o):
        return pltpu.make_async_remote_copy(
            (PS, GPS)[o].at[lax.rem(q + 2, 4), :, pl.ds(half * j, half)], (RH, GRH)[o].at[j],
            rs.at[4 + 4 * o + j], rr.at[4 + 4 * o + j], device_id={"subj": ring((1, 3)[j])}, device_id_type=MESH)

    def zcopy(j, o):
        return pltpu.make_async_remote_copy(
            (PS, GPS)[o].at[lax.rem(q + (1, 3)[j], 4)], (RZ, GRZ)[o].at[j],
            rs.at[6 + 4 * o + j], rr.at[6 + 4 * o + j], device_id={"subj": ring((1, 3)[j])}, device_id_type=MESH)

    def ring_start(o):
        for j in range(2):
            hsum(j, o).start()

    def ring_next(o):
        ref, got = (PS, GPS)[o], (RH, GRH)[o]
        for j in range(2):
            hsum(j, o).wait_recv()
            k = lax.rem(q + (1, 3)[j], 4)
            for z in range(4):
                ref[k, z, pl.ds(half * j, half)] = ref[k, z, pl.ds(half * j, half)] + got[j, z]
            zcopy(j, o).start()

    held_up, held_dn = has_up & (turn == 0), has_dn & (turn == 3)
    free_up, free_dn = has_up & (turn != 0), has_dn & (turn != 3)

    @pl.when(is_guest)
    def _():
        for j in (2, 1, 3):
            gcopy(j).start()

    @pl.when(is_host)
    def _():
        ring_start(0)

    xstart((10, 12, 13, 14), free_up, free_dn)
    smooth(0, 0)

    @pl.when(is_host)
    def _():
        ring_next(0)
        gcopy(2).wait_recv()
        ring_start(1)

    xsent((8,), held_up, held_dn)
    xstart((10,), held_up, held_dn)
    smooth(0, 1)

    @pl.when(is_host)
    def _():
        gcopy(1).wait_recv()
        gcopy(3).wait_recv()
        ring_next(1)

    xstart((12,), held_up, held_dn)
    smooth(0, 2)
    xstart((13, 14), held_up, held_dn)

    @pl.when(is_host)
    def _():
        for o in range(2):
            for j in range(2):
                zcopy(j, o).wait_recv()
        for z in range(4):
            TG2[z] = GRZ[0, z] + GRZ[1, z]
        give_back().start()
        for z in range(4):
            TG[z] = PS[q, z] + RZ[0, z] + RZ[1, z]

    xrecv((4, 5, 6, 8, 9, 10))

    def smooth_1(d, _):
        smooth(1, d)
        return 0

    lax.fori_loop(0, 3, smooth_1, 0)

    @pl.when(is_guest)
    def _():
        give_back().wait_recv()
        for z in range(4):
            TG[z] = PS[q, z] + RZ[0, z]

    tg_copy = pltpu.make_async_copy(TG, tg, ls.at[7])
    tg_copy.start()

    for d in range(3):
        xrecv((12 + d,))

        def fn(r):
            for z, p in ((0, 0), (3, 7)):
                late = at(S.at[0, d, p], r) * (SEVENTH * SEVENTH * SEVENTH)
                out[0, 0, d, z, pl.ds(r, R)] = out[0, 0, d, z, pl.ds(r, R)] + late

        chunks(fn)

    xsent((0, 1, 2, 3, 7, 9, 10, 11, 12, 13, 14, 15, 16, 17))
    xsent((8,), free_up, free_dn)
    for k in range(9):
        tcopy(k).wait_send()
    for j in range(4):
        hcopy(j).wait_send()
    for k in range(4):
        pcopy(k).wait_send()

    @pl.when(is_host)
    def _():
        for o in range(2):
            for j in range(2):
                hsum(j, o).wait_send()
                zcopy(j, o).wait_send()
        give_back().wait_send()

    @pl.when(is_guest)
    def _():
        for j in range(1, 4):
            gcopy(j).wait_send()

    tg_copy.wait()


def write_out(grad_ref, part_ref, grad_out, part_out, sems):
    n = 6
    copies = [pltpu.make_async_copy(part_ref, part_out, sems.at[n])]
    for i in range(n):
        copies.append(pltpu.make_async_copy(grad_ref.at[0, i // 3, i % 3], grad_out.at[0, i // 3, i % 3], sems.at[i]))
    for copy in copies:
        copy.start()
    for copy in copies:
        copy.wait()


def body(nslab, template, subject, velocity):
    depth, blk, nx = template.shape
    ny = subject.shape[2]
    tall = ny + 2 * PAD
    vmem = lambda *shape: pltpu.VMEM(shape, F32)
    dma = lambda *shape: pltpu.SemaphoreType.DMA(shape)
    results = pl.pallas_call(
        functools.partial(kernel, nslab),
        out_shape=(
            jax.ShapeDtypeStruct(velocity.shape, F32),
            jax.ShapeDtypeStruct(template.shape, F32),
        ),
        in_specs=[pl.BlockSpec(memory_space=pltpu.HBM)] * 3,
        out_specs=(pl.BlockSpec(memory_space=pltpu.VMEM), pl.BlockSpec(memory_space=pl.ANY)),
        scratch_shapes=[
            vmem(8, tall, nx),
            vmem(6, tall, nx),
            vmem(4, tall, nx),
            vmem(6, tall, nx),
            vmem(2, 3, 8, tall, nx),
            vmem(6, tall, nx),
            vmem(2, 3, 4, tall, nx),
            vmem(2, 3, ny, nx),
            vmem(4, ny, nx),
            vmem(2, ny, nx),
            vmem(2, ny, nx),
            vmem(4, ny, nx),
            vmem(4, 4, blk, nx),
            vmem(4, 4, blk, nx),
            vmem(2, 4, blk // 2, nx),
            vmem(2, 4, blk, nx),
            vmem(4, blk, nx),
            vmem(4, 4, blk, nx),
            vmem(2, 4, blk // 2, nx),
            vmem(2, 4, blk, nx),
            vmem(4, blk, nx),
            dma(2, 18), dma(2, 18), dma(2, 9), dma(2, 9), dma(12), dma(12), dma(4), dma(4), dma(8),
        ],
        compiler_params=pltpu.CompilerParams(
            collective_id=0, has_side_effects=True, vmem_limit_bytes=40 << 20),
    )(*(pltpu.with_memory_space_constraint(x, pltpu.HBM) for x in (template, subject, velocity)))
    return pl.pallas_call(
        write_out,
        out_shape=(
            jax.ShapeDtypeStruct(velocity.shape, F32),
            jax.ShapeDtypeStruct(template.shape, F32),
        ),
        in_specs=[pl.BlockSpec(memory_space=pltpu.VMEM)] * 2,
        out_specs=(pl.BlockSpec(memory_space=pltpu.HBM),) * 2,
        scratch_shapes=[dma(7)],
        compiler_params=pltpu.CompilerParams(vmem_limit_bytes=16 << 20),
    )(*results)


def solution(mesh):
    return jax.shard_map(
        functools.partial(body, mesh.shape["slab"]),
        mesh=mesh,
        in_specs=(
            P("slab", "subj", None),
            P("subj", "slab", None, None),
            P("subj", None, None, "slab", None, None),
        ),
        out_specs=(P("subj", None, None, "slab", None, None), P("slab", "subj", None)),
        check_vma=False,
    )
```
